32 devices in a mesh: gz: 4 (over z), gy: 2 (over x), vec: 4 (over y, core).
Axes of the slice: x: 2, y: 2, z: 4, core: 2. Of those that a mesh axis runs over, the one named last changes fastest.
Arguments:
- vectors: bfloat16 [256, 3, 32, 4, 128], P('vec', None, 'gz', 'gy'), may hold values from -6 to 6
- links: bfloat16 [3, 3, 3, 32, 4, 128], P(None, None, None, 'gz', 'gy'), may hold values from -4 to 4
- momentum: int32 [3], replicated, may hold values from -5 to 5, as said below
- directions: int32 [3], replicated, may hold values from 0 to 2, each once
Outputs:
- elementals: float32 [4, 2, 256, 256], P(None, None, 'vec')
The draws below stay inside these ranges and needn't reach their ends.
Inputs may be any that keep to these rules, and one draw needn't show every extreme that they name: `momentum`: one component is -5, another 5. `directions`: each of 0, 1, 2 once.
All inputs are finite; a program needn't handle non-finite values.
Results may differ from the reference program's by a relative error of at most 0.0029.
Values may be sent and summed in bfloat16 or wider, within the bound.
A program may use at most 128 MiB of HBM per device.

```python
import math
import jax
import jax.numpy as jnp
from jax import lax

NEV = 256
LX = 64
NY = 4
NZ = 32


def draw_momentum(key, part):
    first_key = jax.random.fold_in(key, 11)
    second_key = jax.random.fold_in(key, 23)
    middle = jax.random.randint(first_key, (1,), -5, 6, dtype=jnp.int32)
    values = jnp.concatenate([jnp.array([-5, 5], dtype=jnp.int32), middle])
    order = jax.random.permutation(second_key, 3)
    return values[order].astype(jnp.int32)


def block_scale(stream_key, extent, cuts, smallest, largest):
    loudness, own = 1.0, jax.random.fold_in(stream_key, 6)
    for position, blocks in cuts:
        heights = jnp.exp(jax.random.uniform(jax.random.fold_in(own, position), (blocks,), jnp.float32, smallest / len(cuts), largest / len(cuts)))
        loudness = loudness * jnp.repeat(heights, extent[position] // blocks).reshape([-1 if axis == position else 1 for axis in range(len(extent))])
    return loudness


def gaussian(stream_key, dims, deviation, bound, pieces=(), kind=jnp.bfloat16):
    factor_of = block_scale(stream_key, dims, pieces, -0.22, 0.18) if pieces else 1.0
    drawn = jax.random.normal(stream_key, dims, jnp.float32) * deviation * factor_of
    return jnp.minimum(jnp.maximum(drawn, -bound), bound).astype(kind)


def setup_inputs(seed: int = 0) -> dict:
    arg_keys = jax.random.split(jax.random.key(seed), 5)
    return {
        "vectors": gaussian(arg_keys[0], (NEV, 3, NZ, NY, 2 * LX), 1.0, 6.0, ((0, 4), (2, 4), (3, 2))),
        "links": gaussian(arg_keys[1], (3, 3, 3, NZ, NY, 2 * LX), 0.58, 4.0, ((3, 4), (4, 2))),
        "momentum": draw_momentum(jax.random.fold_in(arg_keys[4], 71), 0),
        "directions": jax.random.permutation(arg_keys[3], 3).astype(jnp.int32),
    }


def apply_link(link_pair, field_pair):
    link_real, link_imag = link_pair
    field_real, field_imag = field_pair
    out_real = 0.0
    out_imag = 0.0
    for column in range(3):
        coeff_real = link_real[:, column][None]
        coeff_imag = link_imag[:, column][None]
        value_real = field_real[:, column][:, None]
        value_imag = field_imag[:, column][:, None]
        out_real = out_real + coeff_real * value_real - coeff_imag * value_imag
        out_imag = out_imag + coeff_real * value_imag + coeff_imag * value_real
    return (out_real, out_imag)

def apply_adjoint(link_pair, field_pair):
    link_real, link_imag = link_pair
    field_real, field_imag = field_pair
    out_real = 0.0
    out_imag = 0.0
    for column in range(3):
        coeff_real = link_real[column][None]
        coeff_imag = link_imag[column][None]
        value_real = field_real[:, column][:, None]
        value_imag = field_imag[:, column][:, None]
        out_real = out_real + coeff_real * value_real + coeff_imag * value_imag
        out_imag = out_imag + coeff_real * value_imag - coeff_imag * value_real
    return (out_real, out_imag)

def covariant(up_pair, down_pair, ahead_pair, behind_pair):
    forward = apply_link(up_pair, ahead_pair)
    backward = apply_adjoint(down_pair, behind_pair)
    return (0.5 * (forward[0] - backward[0]), 0.5 * (forward[1] - backward[1]))

def phase_table(momentum, x_coords, y_coords, z_coords, extent_x, extent_y, extent_z):
    frac_x = (momentum[0] * x_coords % extent_x).astype(jnp.float32) / extent_x
    frac_y = (momentum[1] * y_coords % extent_y).astype(jnp.float32) / extent_y
    frac_z = (momentum[2] * z_coords % extent_z).astype(jnp.float32) / extent_z
    summed = frac_z[:, None, None] + frac_y[None, :, None] + frac_x[None, None, :]
    angle = 2.0 * math.pi * summed
    return (jnp.cos(angle), jnp.sin(angle))

def make_operators(field_pair, ahead_list, behind_list, up_list, down_list, directions, cosine, sine):
    derived = [covariant(up_list[axis_number], down_list[axis_number], ahead_list[axis_number], behind_list[axis_number]) for axis_number in range(3)]
    results = []
    for op_slot in range(3):
        chosen = directions[op_slot]
        real_part = jnp.where(chosen == 0, derived[0][0], jnp.where(chosen == 1, derived[1][0], derived[2][0]))
        imag_part = jnp.where(chosen == 0, derived[0][1], jnp.where(chosen == 1, derived[1][1], derived[2][1]))
        results.append(jnp.stack([real_part, imag_part], -2).astype(jnp.bfloat16))
    field_real, field_imag = field_pair
    phased_real = field_real * cosine + field_imag * sine
    phased_imag = field_imag * cosine - field_real * sine
    results.append(jnp.stack([phased_real, phased_imag], -2).astype(jnp.bfloat16))
    return jnp.stack(results, 1)

def contract(rows, stacked_left):
    row_count = rows.shape[0]
    flat_rows = rows.reshape(row_count * 4, -1)
    product = lax.dot_general(flat_rows, stacked_left, (((1,), (1,)), ((), ())), preferred_element_type=jnp.float32)
    return product.reshape(row_count, 4, 2, stacked_left.shape[0] // 2)

def reference(vectors, links, momentum, directions):
    six_dims = vectors.reshape(NEV, 3, NZ, NY, 2, LX)
    swapped = jnp.stack([-six_dims[..., 1, :], six_dims[..., 0, :]], -2)
    stacked_left = jnp.concatenate([vectors.reshape(NEV, -1), swapped.reshape(NEV, -1)], 0)
    link_wide = links.astype(jnp.float32).reshape(3, 3, 3, NZ, NY, 2, LX)
    up_list = [(link_wide[axis_number, ..., 0, :], link_wide[axis_number, ..., 1, :]) for axis_number in range(3)]
    down_list = [(jnp.roll(up_list[axis_number][0], 1, axis=-1 - axis_number), jnp.roll(up_list[axis_number][1], 1, axis=-1 - axis_number)) for axis_number in range(3)]
    cosine, sine = phase_table(momentum, jnp.arange(LX, dtype=jnp.int32), jnp.arange(NY, dtype=jnp.int32), jnp.arange(NZ, dtype=jnp.int32), LX, NY, NZ)
    block_size = NEV // 16

    def one_block(block_index):
        first_row = (block_index * block_size).astype(jnp.int32)
        block = lax.dynamic_slice_in_dim(vectors, first_row, block_size, 0)
        widened = block.astype(jnp.float32).reshape(block_size, 3, NZ, NY, 2, LX)
        field_real = widened[..., 0, :]
        field_imag = widened[..., 1, :]
        ahead_list = [(jnp.roll(field_real, -1, axis=-1 - axis_number), jnp.roll(field_imag, -1, axis=-1 - axis_number)) for axis_number in range(3)]
        behind_list = [(jnp.roll(field_real, 1, axis=-1 - axis_number), jnp.roll(field_imag, 1, axis=-1 - axis_number)) for axis_number in range(3)]
        transformed = make_operators((field_real, field_imag), ahead_list, behind_list, up_list, down_list, directions, cosine, sine)
        return contract(transformed.reshape(block_size, 4, -1), stacked_left)
    blocks = lax.map(one_block, jnp.arange(16, dtype=jnp.int32))
    summed = blocks.reshape(NEV, 4, 2, NEV) * (1.0 / math.sqrt(LX * NY * NZ))
    return jnp.transpose(summed, (1, 2, 0, 3))
```

```python
import functools
import math

import jax
import jax.numpy as jnp
from jax import lax
from jax.experimental import pallas as pl
from jax.experimental.pallas import tpu as pltpu
from jax.sharding import PartitionSpec as P

MESH = pl.DeviceIdType.MESH


def split_chunks(depth, most):
    count = most
    while depth % count:
        count -= 1
    return count


def kernel(
    sizes,
    v_ref,
    tabx_ref,
    taby_ref,
    tabz_ref,
    phase_ref,
    out_ref,
    ext,
    left,
    ty,
    tz,
    trans,
    acc,
    outgo,
    income,
    reduced,
    local_sem,
    send_sem,
    recv_sem,
    red_sem,
):
    gz_n, gy_n, vec_n, depth, height, rows, width, chunks = sizes
    pairs = vec_n // 2
    lanes = 2 * width
    me_z = lax.axis_index("gz")
    me_y = lax.axis_index("gy")
    me_v = lax.axis_index("vec")
    pair = me_v // 2
    side = lax.rem(me_v, 2)
    group = gz_n * gy_n
    me_g = me_z * gy_n + me_y

    def member(step):
        return lax.rem(me_g + step, group)

    def place(g):
        return {"gz": g // gy_n, "gy": lax.rem(g, gy_n)}

    centre = ext.at[pl.ds(1, depth), pl.ds(1, height)]
    locals_ = [
        pltpu.make_async_copy(v_ref, centre, local_sem.at[0]),
        pltpu.make_async_copy(v_ref, left.at[pair, side], local_sem.at[1]),
        pltpu.make_async_copy(taby_ref, ty.at[:, pl.ds(1, height)], local_sem.at[2]),
        pltpu.make_async_copy(tabz_ref, tz.at[pl.ds(1, depth)], local_sem.at[3]),
    ]
    for copy in locals_:
        copy.start()

    barrier = pltpu.get_barrier_semaphore()
    for step in range(1, group):
        pl.semaphore_signal(barrier, inc=1, device_id=place(member(step)), device_id_type=MESH)
    for step in range(1, vec_n):
        pl.semaphore_signal(
            barrier, inc=1, device_id={"vec": lax.rem(me_v + step, vec_n)}, device_id_type=MESH
        )
    pl.semaphore_wait(barrier, group - 1 + vec_n - 1)

    counter = [0]

    def remote(src, dst, device):
        index = counter[0]
        counter[0] += 1
        return pltpu.make_async_remote_copy(
            src_ref=src,
            dst_ref=dst,
            send_sem=send_sem.at[index],
            recv_sem=recv_sem.at[index],
            device_id=device,
            device_id_type=MESH,
        )

    z_up = {"gz": lax.rem(me_z + 1, gz_n)}
    z_down = {"gz": lax.rem(me_z + gz_n - 1, gz_n)}
    y_up = {"gy": lax.rem(me_y + 1, gy_n)}
    y_down = {"gy": lax.rem(me_y + gy_n - 1, gy_n)}
    sibling = {"vec": pair * 2 + 1 - side}
    inner_z = pl.ds(1, depth)
    inner_y = pl.ds(1, height)
    z_copies = [
        remote(v_ref.at[depth - 1], ext.at[0, inner_y], z_up),
        remote(v_ref.at[0], ext.at[depth + 1, inner_y], z_down),
        remote(tabz_ref.at[depth - 1], tz.at[0], z_up),
    ]
    y_copies = [
        remote(v_ref.at[:, height - 1], ext.at[inner_z, 0], y_up),
        remote(v_ref.at[:, 0], ext.at[inner_z, height + 1], y_down),
        remote(taby_ref.at[:, height - 1], ty.at[:, 0], y_up),
    ]
    near = remote(v_ref, left.at[pair, side], sibling)
    span = depth // chunks
    far = []
    relay = []
    for k in range(chunks):
        part = pl.ds(k * span, span)
        for hop in range(1, pairs):
            target = lax.rem(pair + hop, pairs)
            source = lax.rem(pair + pairs - hop, pairs)
            far.append(
                remote(
                    v_ref.at[part], left.at[pair, side, part], {"vec": target * 2 + side}
                )
            )
            relay.append(
                remote(left.at[source, side, part], left.at[source, side, part], sibling)
            )
    for copy in z_copies:
        copy.start()
    for copy in far[: pairs - 1]:
        copy.start()
    for copy in y_copies:
        copy.start()
    for copy in far[pairs - 1 :]:
        copy.start()
    near.start()

    lane = lax.broadcasted_iota(jnp.int32, (1, lanes), 1)
    last_mask = lax.rem(lane, width) == width - 1
    first_mask = lax.rem(lane, width) == 0
    sign = jnp.where(lane < width, 1.0, -1.0).astype(jnp.float32)
    tile = 32 if rows % 32 == 0 else rows

    def store(z, y, colour, slot, lo, value):
        turned = pltpu.roll(value, width, 1) * sign
        trans[z, y, colour, pl.ds(slot * 2 * rows + lo, tile)] = value.astype(jnp.bfloat16)
        trans[z, y, colour, pl.ds((slot * 2 + 1) * rows + lo, tile)] = turned.astype(jnp.bfloat16)

    def load(z, y, colour, lo):
        return ext[z, y, colour, pl.ds(lo, tile)].astype(jnp.float32)

    def stencil(z, y, lo, slot, ahead, behind, up, down):
        sums = [0.0, 0.0, 0.0]
        for col in range(3):
            value, swapped = ahead(col)
            for row in range(3):
                k = row * 3 + col
                sums[row] = sums[row] + (up(k) * value + up(9 + k) * swapped)
        for col in range(3):
            value, swapped = behind(col)
            for row in range(3):
                k = col * 3 + row
                sums[row] = sums[row] + (down(9 + k) * swapped - down(k) * value)
        for row in range(3):
            store(z, y, row, slot, lo, sums[row])

    def swap(value):
        return value, pltpu.roll(value, width, 1)

    def pass_x(z):
        for y in range(height):
            for lo in range(0, rows, tile):
                cosine = phase_ref[z, y, 0:1]
                sine = phase_ref[z, y, 1:2]

                def ahead(col):
                    value = load(z + 1, y + 1, col, lo)
                    one = pltpu.roll(value, lanes - 1, 1)
                    two = pltpu.roll(value, width - 1, 1)
                    return jnp.where(last_mask, two, one), jnp.where(last_mask, one, two)

                def behind(col):
                    value = load(z + 1, y + 1, col, lo)
                    one = pltpu.roll(value, 1, 1)
                    two = pltpu.roll(value, width + 1, 1)
                    return jnp.where(first_mask, two, one), jnp.where(first_mask, one, two)

                stencil(
                    z, y, lo, 0, ahead, behind,
                    lambda k: tabx_ref[0, z, y, k : k + 1],
                    lambda k: tabx_ref[1, z, y, k : k + 1],
                )
                for col in range(3):
                    value, swapped = swap(load(z + 1, y + 1, col, lo))
                    store(z, y, col, 3, lo, value * cosine + swapped * sine)

    def pass_y(z):
        for y in range(height):
            for lo in range(0, rows, tile):
                stencil(
                    z, y, lo, 1,
                    lambda col: swap(load(z + 1, y + 2, col, lo)),
                    lambda col: swap(load(z + 1, y, col, lo)),
                    lambda k: ty[z, y + 1, k : k + 1],
                    lambda k: ty[z, y, k : k + 1],
                )

    def pass_z(z):
        for y in range(height):
            for lo in range(0, rows, tile):
                stencil(
                    z, y, lo, 2,
                    lambda col: swap(load(z + 2, y + 1, col, lo)),
                    lambda col: swap(load(z, y + 1, col, lo)),
                    lambda k: tz[z + 1, y, k : k + 1],
                    lambda k: tz[z, y, k : k + 1],
                )

    for copy in locals_:
        copy.wait()
    pl.loop(0, depth)(pass_x)
    for copy in z_copies:
        copy.wait()
    pl.loop(0, depth)(pass_z)
    for copy in y_copies:
        copy.wait()
    pl.loop(0, depth)(pass_y)

    share = 8 * rows // group

    def contract(which, z, fresh):
        sites = [(y, c) for y in range(height) for c in range(3)]
        a = jnp.concatenate([trans[z, y, c] for y, c in sites], axis=1)
        b = jnp.concatenate(
            [
                jnp.concatenate([left[which, s, z, y, c] for y, c in sites], axis=1)
                for s in range(2)
            ],
            axis=0,
        )
        product = lax.dot_general(
            a, b, (((1,), (1,)), ((), ())), preferred_element_type=jnp.float32
        ).reshape(group, share, 2 * rows)
        columns = pl.ds(pl.multiple_of(which * 2 * rows, 2 * rows), 2 * rows)
        if fresh:
            acc[:, :, columns] = product
        else:
            acc[:, :, columns] += product

    def contract_range(which, lo, hi):
        start = lo
        if lo == 0:
            contract(which, 0, True)
            start = 1
        if hi > start:
            pl.loop(start, hi)(lambda z: contract(which, z, False))

    near.wait()
    contract_range(pair, 0, depth)
    for k in range(chunks):
        for hop in range(1, pairs):
            index = k * (pairs - 1) + hop - 1
            far[index].wait()
            relay[index].start()
        if k:
            for hop in range(1, pairs):
                relay[(k - 1) * (pairs - 1) + hop - 1].wait()
                contract_range(
                    lax.rem(pair + pairs - hop, pairs), (k - 1) * span, k * span
                )
    for hop in range(1, pairs):
        relay[(chunks - 1) * (pairs - 1) + hop - 1].wait()
        contract_range(lax.rem(pair + pairs - hop, pairs), (chunks - 1) * span, depth)

    outgo[...] = acc[...].astype(jnp.bfloat16)
    scatter = []
    for step in range(1, group):
        g = member(step)
        copy = pltpu.make_async_remote_copy(
            src_ref=outgo.at[g],
            dst_ref=income.at[me_g],
            send_sem=red_sem.at[0, step],
            recv_sem=red_sem.at[1, step],
            device_id=place(g),
            device_id_type=MESH,
        )
        copy.start()
        scatter.append(copy)
    for copy in scatter:
        copy.wait()
    total = acc[me_g]
    for step in range(1, group):
        total = total + income[member(step)].astype(jnp.float32)
    reduced[...] = total.astype(jnp.bfloat16)
    out_ref[me_g] = total.astype(jnp.bfloat16)
    gather = []
    for step in range(1, group):
        g = member(step)
        copy = pltpu.make_async_remote_copy(
            src_ref=reduced,
            dst_ref=out_ref.at[me_g],
            send_sem=red_sem.at[2, step],
            recv_sem=red_sem.at[3, step],
            device_id=place(g),
            device_id_type=MESH,
        )
        copy.start()
        gather.append(copy)
    for copy in gather:
        copy.wait()


def link_table(real, imag):
    first = jnp.concatenate([real, real], -1)
    second = jnp.concatenate([-imag, imag], -1)
    both = jnp.stack([first, second], 0) * 0.5
    both = jnp.transpose(both, (3, 4, 0, 1, 2, 5))
    depth, height = both.shape[:2]
    return both.reshape(depth, height, 18, both.shape[-1])


def body(vectors, links, momentum, directions):
    rows, _, depth, height, lanes = vectors.shape
    width = lanes // 2
    gz_n = lax.axis_size("gz")
    gy_n = lax.axis_size("gy")
    vec_n = lax.axis_size("vec")
    group = gz_n * gy_n
    extent_y = height * gy_n
    extent_z = depth * gz_n
    chunks = split_chunks(depth, 4)

    v = jnp.transpose(vectors, (2, 3, 1, 0, 4))
    wide = links.astype(jnp.float32).reshape(3, 3, 3, depth, height, 2, width)
    real = wide[..., 0, :]
    imag = wide[..., 1, :]
    tabx = jnp.stack(
        [
            link_table(real[0], imag[0]),
            link_table(jnp.roll(real[0], 1, -1), jnp.roll(imag[0], 1, -1)),
        ]
    )
    taby = link_table(real[1], imag[1])
    tabz = link_table(real[2], imag[2])

    x = jnp.arange(width, dtype=jnp.int32)
    y = lax.axis_index("gy") * height + jnp.arange(height, dtype=jnp.int32)
    z = lax.axis_index("gz") * depth + jnp.arange(depth, dtype=jnp.int32)
    frac_x = (momentum[0] * x % width).astype(jnp.float32) / width
    frac_y = (momentum[1] * y % extent_y).astype(jnp.float32) / extent_y
    frac_z = (momentum[2] * z % extent_z).astype(jnp.float32) / extent_z
    summed = frac_z[:, None, None] + frac_y[None, :, None] + frac_x[None, None, :]
    angle = 2.0 * math.pi * summed
    cosine, sine = jnp.cos(angle), jnp.sin(angle)
    phase = jnp.stack(
        [jnp.concatenate([cosine, cosine], -1), jnp.concatenate([sine, -sine], -1)], 2
    )

    share = 8 * rows // group
    bf16, f32 = jnp.bfloat16, jnp.float32
    remote_count = 7 + 2 * chunks * (vec_n // 2 - 1)
    vmem = pl.BlockSpec(memory_space=pltpu.VMEM)
    hbm = pl.BlockSpec(memory_space=pl.ANY)
    sizes = (gz_n, gy_n, vec_n, depth, height, rows, width, chunks)
    out = pl.pallas_call(
        functools.partial(kernel, sizes),
        out_shape=jax.ShapeDtypeStruct((group, share, vec_n * rows), bf16),
        in_specs=[hbm, vmem, hbm, hbm, vmem],
        out_specs=vmem,
        scratch_shapes=[
            pltpu.VMEM((depth + 2, height + 2, 3, rows, lanes), bf16),
            pltpu.VMEM((vec_n // 2, 2, depth, height, 3, rows, lanes), bf16),
            pltpu.VMEM((depth, height + 1, 18, lanes), f32),
            pltpu.VMEM((depth + 1, height, 18, lanes), f32),
            pltpu.VMEM((depth, height, 3, 8 * rows, lanes), bf16),
            pltpu.VMEM((group, share, vec_n * rows), f32),
            pltpu.VMEM((group, share, vec_n * rows), bf16),
            pltpu.VMEM((group, share, vec_n * rows), bf16),
            pltpu.VMEM((share, vec_n * rows), bf16),
            pltpu.SemaphoreType.DMA((4,)),
            pltpu.SemaphoreType.DMA((remote_count,)),
            pltpu.SemaphoreType.DMA((remote_count,)),
            pltpu.SemaphoreType.DMA((4, group)),
        ],
        compiler_params=pltpu.CompilerParams(
            collective_id=0, has_side_effects=True, vmem_limit_bytes=48 * 1024 * 1024
        ),
    )(v, tabx, taby, tabz, phase)

    scale = 1.0 / math.sqrt(width * extent_y * extent_z)
    derived = out.reshape(4, 2, rows, vec_n * rows)
    parts = []
    for slot in range(3):
        chosen = directions[slot]
        parts.append(
            jnp.where(chosen == 0, derived[0], jnp.where(chosen == 1, derived[1], derived[2]))
        )
    parts.append(derived[3])
    return jnp.stack(parts).astype(f32) * scale


def solution(mesh):
    in_specs = (P("vec", None, "gz", "gy", None), P(None, None, None, "gz", "gy", None), P(), P())
    out_specs = P(None, None, "vec", None)
    return jax.shard_map(body, mesh=mesh, in_specs=in_specs, out_specs=out_specs, check_vma=False)
```

```python
import functools
import math

import jax
import jax.numpy as jnp
from jax import lax
from jax.experimental import pallas as pl
from jax.experimental.pallas import tpu as pltpu
from jax.sharding import PartitionSpec as P

MESH = pl.DeviceIdType.MESH


def split_chunks(depth, most):
    count = most
    while depth % count:
        count -= 1
    return count


def kernel(
    sizes,
    momentum_ref,
    directions_ref,
    v_ref,
    links_ref,
    links_far,
    out_ref,
    ext,
    left,
    rim_y,
    rim_z,
    tab_x,
    tab_y,
    tab_z,
    cos_ref,
    sin_ref,
    trans,
    acc,
    outgo,
    income,
    reduced,
    gathered,
    local_sem,
    send_sem,
    recv_sem,
    red_sem,
):
    gz_n, gy_n, vec_n, depth, height, rows, width, chunks = sizes
    pairs = vec_n // 2
    lanes = 2 * width
    me_z = lax.axis_index("gz")
    me_y = lax.axis_index("gy")
    me_v = lax.axis_index("vec")
    pair = me_v // 2
    side = lax.rem(me_v, 2)
    group = gz_n * gy_n
    me_g = me_z * gy_n + me_y
    span = depth // chunks

    def member(step):
        return lax.rem(me_g + step, group)

    def place(g):
        return {"gz": g // gy_n, "gy": lax.rem(g, gy_n)}

    barrier = pltpu.get_barrier_semaphore()
    for step in range(1, group):
        pl.semaphore_signal(barrier, inc=1, device_id=place(member(step)), device_id_type=MESH)
    for step in range(1, vec_n):
        pl.semaphore_signal(
            barrier, inc=1, device_id={"vec": lax.rem(me_v + step, vec_n)}, device_id_type=MESH
        )
    centre = ext.at[pl.ds(1, depth), pl.ds(1, height)]
    locals_ = [
        pltpu.make_async_copy(v_ref, centre, local_sem.at[0]),
        pltpu.make_async_copy(v_ref, left.at[pair, side], local_sem.at[1]),
    ]
    for copy in locals_:
        copy.start()
    pl.semaphore_wait(barrier, group - 1 + vec_n - 1)

    counter = [0]

    def remote(src, dst, device):
        index = counter[0]
        counter[0] += 1
        return pltpu.make_async_remote_copy(
            src_ref=src,
            dst_ref=dst,
            send_sem=send_sem.at[index],
            recv_sem=recv_sem.at[index],
            device_id=device,
            device_id_type=MESH,
        )

    z_up = {"gz": lax.rem(me_z + 1, gz_n)}
    z_down = {"gz": lax.rem(me_z + gz_n - 1, gz_n)}
    y_up = {"gy": lax.rem(me_y + 1, gy_n)}
    y_down = {"gy": lax.rem(me_y + gy_n - 1, gy_n)}
    sibling = {"vec": pair * 2 + 1 - side}
    inner_y = pl.ds(1, height)
    z_copies = [
        remote(v_ref.at[depth - 1], ext.at[0, inner_y], z_up),
        remote(v_ref.at[0], ext.at[depth + 1, inner_y], z_down),
        remote(links_far.at[2, depth - 1], rim_z, z_up),
    ]
    rim_copy = remote(links_far.at[1, :, height - 1], rim_y, y_up)
    near = remote(v_ref, left.at[pair, side], sibling)
    far, relay, y_copies = [], [], []
    for k in range(chunks):
        part = pl.ds(k * span, span)
        inner_z = pl.ds(1 + k * span, span)
        y_copies.append(
            (
                remote(v_ref.at[part, height - 1], ext.at[inner_z, 0], y_up),
                remote(v_ref.at[part, 0], ext.at[inner_z, height + 1], y_down),
            )
        )
        for hop in range(1, pairs):
            target = lax.rem(pair + hop, pairs)
            source = lax.rem(pair + pairs - hop, pairs)
            far.append(
                remote(v_ref.at[part], left.at[pair, side, part], {"vec": target * 2 + side})
            )
            relay.append(
                remote(left.at[source, side, part], left.at[source, side, part], sibling)
            )
    rim_copy.start()
    for copy in z_copies:
        copy.start()
    for k in range(chunks):
        for copy in far[k * (pairs - 1) : (k + 1) * (pairs - 1)]:
            copy.start()
        for copy in y_copies[k]:
            copy.start()
    near.start()

    lane = lax.broadcasted_iota(jnp.int32, (1, lanes), 1)
    low_half = lane < width
    last_mask = lax.rem(lane, width) == width - 1
    first_mask = lax.rem(lane, width) == 0
    sign = jnp.where(low_half, 1.0, -1.0).astype(jnp.float32)
    tile = 32 if rows % 32 == 0 else rows

    site_shape = (depth * height, lanes)
    site = lax.broadcasted_iota(jnp.int32, site_shape, 0)
    x_at = lax.rem(lax.broadcasted_iota(jnp.int32, site_shape, 1), width)
    y_at = me_y * height + lax.rem(site, height)
    z_at = me_z * depth + site // height

    def fraction(component, at, extent):
        turned = lax.rem(momentum_ref[component] * at, extent)
        turned = jnp.where(turned < 0, turned + extent, turned)
        return turned.astype(jnp.float32) / extent

    angle = (2.0 * math.pi) * (
        fraction(2, z_at, depth * gz_n)
        + fraction(1, y_at, height * gy_n)
        + fraction(0, x_at, width)
    )
    cos_ref[...] = jnp.cos(angle)
    sin_ref[...] = jnp.sin(angle) * sign

    def coefficients(raw):
        value = raw.astype(jnp.float32) * 0.5
        swapped = pltpu.roll(value, width, 1)
        real = jnp.where(low_half, value, swapped)
        imag = jnp.where(low_half, -swapped, value)
        return real, imag

    def put(table, where, pair_of):
        table[where + (slice(0, 9),)] = pair_of[0]
        table[where + (slice(16, 25),)] = pair_of[1]

    def step_back(value):
        one = pltpu.roll(value, 1, 1)
        two = pltpu.roll(value, width + 1, 1)
        return jnp.where(first_mask, two, one)

    def make_tables(z):
        for y in range(height):
            real, imag = coefficients(links_ref[0, z, y])
            put(tab_x, (0, z, y), (real, imag))
            put(tab_x, (1, z, y), (step_back(real), step_back(imag)))
            put(tab_y, (z, y + 1), coefficients(links_ref[1, z, y]))
            put(tab_z, (z + 1, y), coefficients(links_ref[2, z, y]))

    pl.loop(0, depth)(make_tables)

    def store(z, y, colour, slot, lo, value):
        turned = pltpu.roll(value, width, 1) * sign
        trans[z, y, colour, pl.ds(slot * 2 * rows + lo, tile)] = value.astype(jnp.bfloat16)
        trans[z, y, colour, pl.ds((slot * 2 + 1) * rows + lo, tile)] = turned.astype(jnp.bfloat16)

    def load(z, y, colour, lo):
        return ext[z, y, colour, pl.ds(lo, tile)].astype(jnp.float32)

    def stencil(z, y, lo, slot, ahead, behind, up, down):
        sums = [0.0, 0.0, 0.0]
        for col in range(3):
            value, swapped = ahead(col)
            for row in range(3):
                k = row * 3 + col
                sums[row] = sums[row] + (up(k) * value + up(16 + k) * swapped)
        for col in range(3):
            value, swapped = behind(col)
            for row in range(3):
                k = col * 3 + row
                sums[row] = sums[row] + (down(16 + k) * swapped - down(k) * value)
        for row in range(3):
            store(z, y, row, slot, lo, sums[row])

    def swap(value):
        return value, pltpu.roll(value, width, 1)

    def pass_x(z):
        for y in range(height):
            for lo in range(0, rows, tile):
                here = pl.ds(z * height + y, 1)
                cosine = cos_ref[here]
                sine = sin_ref[here]

                def ahead(col):
                    value = load(z + 1, y + 1, col, lo)
                    one = pltpu.roll(value, lanes - 1, 1)
                    two = pltpu.roll(value, width - 1, 1)
                    return jnp.where(last_mask, two, one), jnp.where(last_mask, one, two)

                def behind(col):
                    value = load(z + 1, y + 1, col, lo)
                    one = pltpu.roll(value, 1, 1)
                    two = pltpu.roll(value, width + 1, 1)
                    return jnp.where(first_mask, two, one), jnp.where(first_mask, one, two)

                stencil(
                    z, y, lo, 0, ahead, behind,
                    lambda k: tab_x[0, z, y, k : k + 1],
                    lambda k: tab_x[1, z, y, k : k + 1],
                )
                for col in range(3):
                    value, swapped = swap(load(z + 1, y + 1, col, lo))
                    store(z, y, col, 2, lo, value * cosine + swapped * sine)

    def pass_y(z):
        for y in range(height):
            for lo in range(0, rows, tile):
                stencil(
                    z, y, lo, 3,
                    lambda col: swap(load(z + 1, y + 2, col, lo)),
                    lambda col: swap(load(z + 1, y, col, lo)),
                    lambda k: tab_y[z, y + 1, k : k + 1],
                    lambda k: tab_y[z, y, k : k + 1],
                )

    def pass_z(z):
        for y in range(height):
            for lo in range(0, rows, tile):
                stencil(
                    z, y, lo, 1,
                    lambda col: swap(load(z + 2, y + 1, col, lo)),
                    lambda col: swap(load(z, y + 1, col, lo)),
                    lambda k: tab_z[z + 1, y, k : k + 1],
                    lambda k: tab_z[z, y, k : k + 1],
                )

    def contract(which, chunk, lo, hi, fresh):
        sites = [
            (chunk * span + dz, y, c) for dz in range(span) for y in range(height) for c in range(3)
        ]
        a = jnp.concatenate([trans[z, y, c, lo:hi] for z, y, c in sites], axis=1)
        b = jnp.concatenate(
            [
                jnp.concatenate([left[which, s, z, y, c] for z, y, c in sites], axis=1)
                for s in range(2)
            ],
            axis=0,
        )
        product = lax.dot_general(
            a, b, (((1,), (1,)), ((), ())), preferred_element_type=jnp.float32
        )
        columns = pl.ds(pl.multiple_of(which * 2 * rows, 2 * rows), 2 * rows)
        if fresh:
            acc[lo:hi, columns] = product
        else:
            acc[lo:hi, columns] += product

    for copy in locals_:
        copy.wait()
    pl.loop(0, depth)(pass_x)
    for copy in z_copies:
        copy.wait()
    for y in range(height):
        put(tab_z, (0, y), coefficients(rim_z[y]))
    pl.loop(0, depth)(pass_z)

    early = 6 * rows
    near.wait()
    contract(pair, 0, 0, early, True)
    pl.loop(1, chunks)(lambda k: contract(pair, k, 0, early, False))

    rim_copy.wait()

    @pl.loop(0, depth)
    def _(z):
        put(tab_y, (z, 0), coefficients(rim_y[z]))

    for k in range(chunks + 1):
        if k < chunks:
            for copy in y_copies[k]:
                copy.wait()
            pl.loop(k * span, (k + 1) * span)(pass_y)
            contract(pair, k, early, 8 * rows, k == 0)
            for hop in range(1, pairs):
                index = k * (pairs - 1) + hop - 1
                far[index].wait()
                relay[index].start()
        if k:
            for hop in range(1, pairs):
                relay[(k - 1) * (pairs - 1) + hop - 1].wait()
                contract(lax.rem(pair + pairs - hop, pairs), k - 1, 0, 8 * rows, k == 1)

    share = 8 * rows // group
    outgo[...] = acc[...].reshape(outgo.shape).astype(jnp.bfloat16)
    scatter = []
    for step in range(1, group):
        g = member(step)
        copy = pltpu.make_async_remote_copy(
            src_ref=outgo.at[g],
            dst_ref=income.at[me_g],
            send_sem=red_sem.at[0, step],
            recv_sem=red_sem.at[1, step],
            device_id=place(g),
            device_id_type=MESH,
        )
        copy.start()
        scatter.append(copy)
    for copy in scatter:
        copy.wait()
    total = acc[pl.ds(pl.multiple_of(me_g * share, share), share)]
    for step in range(1, group):
        total = total + income[member(step)].astype(jnp.float32)
    reduced[...] = total.astype(jnp.bfloat16)
    gathered[me_g] = total.astype(jnp.bfloat16)
    gather = []
    for step in range(1, group):
        g = member(step)
        copy = pltpu.make_async_remote_copy(
            src_ref=reduced,
            dst_ref=gathered.at[me_g],
            send_sem=red_sem.at[2, step],
            recv_sem=red_sem.at[3, step],
            device_id=place(g),
            device_id_type=MESH,
        )
        copy.start()
        gather.append(copy)
    for copy in gather:
        copy.wait()

    scale = 1.0 / math.sqrt(width * height * gy_n * depth * gz_n)
    full = gathered[...].astype(jnp.float32).reshape(8 * rows, vec_n * rows) * scale
    along_x, along_z, phased, along_y = [
        full[slot * 2 * rows : (slot + 1) * 2 * rows] for slot in range(4)
    ]
    for slot in range(3):
        chosen = directions_ref[slot]
        out_ref[slot * 2 * rows : (slot + 1) * 2 * rows] = jnp.where(
            chosen == 0, along_x, jnp.where(chosen == 1, along_y, along_z)
        )
    out_ref[6 * rows :] = phased


def body(vectors, links, momentum, directions):
    rows, _, depth, height, lanes = vectors.shape
    gz_n = lax.axis_size("gz")
    gy_n = lax.axis_size("gy")
    vec_n = lax.axis_size("vec")
    group = gz_n * gy_n
    chunks = split_chunks(depth, 4)
    v = jnp.transpose(vectors, (2, 3, 1, 0, 4))
    packed = jnp.transpose(links, (0, 3, 4, 1, 2, 5)).reshape(3, depth, height, 9, lanes)

    share = 8 * rows // group
    bf16, f32 = jnp.bfloat16, jnp.float32
    pairs = vec_n // 2
    remote_count = 5 + chunks * (2 + 2 * (pairs - 1))
    vmem = pl.BlockSpec(memory_space=pltpu.VMEM)
    smem = pl.BlockSpec(memory_space=pltpu.SMEM)
    hbm = pl.BlockSpec(memory_space=pl.ANY)
    sizes = (gz_n, gy_n, vec_n, depth, height, rows, lanes // 2, chunks)
    out = pl.pallas_call(
        functools.partial(kernel, sizes),
        out_shape=jax.ShapeDtypeStruct((8 * rows, vec_n * rows), f32),
        in_specs=[smem, smem, hbm, vmem, hbm],
        out_specs=vmem,
        scratch_shapes=[
            pltpu.VMEM((depth + 2, height + 2, 3, rows, lanes), bf16),
            pltpu.VMEM((pairs, 2, depth, height, 3, rows, lanes), bf16),
            pltpu.VMEM((depth, 9, lanes), bf16),
            pltpu.VMEM((height, 9, lanes), bf16),
            pltpu.VMEM((2, depth, height, 32, lanes), f32),
            pltpu.VMEM((depth, height + 1, 32, lanes), f32),
            pltpu.VMEM((depth + 1, height, 32, lanes), f32),
            pltpu.VMEM((depth * height, lanes), f32),
            pltpu.VMEM((depth * height, lanes), f32),
            pltpu.VMEM((depth, height, 3, 8 * rows, lanes), bf16),
            pltpu.VMEM((8 * rows, vec_n * rows), f32),
            pltpu.VMEM((group, share, vec_n * rows), bf16),
            pltpu.VMEM((group, share, vec_n * rows), bf16),
            pltpu.VMEM((share, vec_n * rows), bf16),
            pltpu.VMEM((group, share, vec_n * rows), bf16),
            pltpu.SemaphoreType.DMA((2,)),
            pltpu.SemaphoreType.DMA((remote_count,)),
            pltpu.SemaphoreType.DMA((remote_count,)),
            pltpu.SemaphoreType.DMA((4, group)),
        ],
        compiler_params=pltpu.CompilerParams(
            collective_id=0, has_side_effects=True, vmem_limit_bytes=48 * 1024 * 1024
        ),
    )(momentum, directions, v, packed, packed)
    return out.reshape(4, 2, rows, vec_n * rows)


def solution(mesh):
    in_specs = (P("vec", None, "gz", "gy", None), P(None, None, None, "gz", "gy", None), P(), P())
    out_specs = P(None, None, "vec", None)
    return jax.shard_map(body, mesh=mesh, in_specs=in_specs, out_specs=out_specs, check_vma=False)
```

```python
import functools
import math

import jax
import jax.numpy as jnp
from jax import lax
from jax.experimental import pallas as pl
from jax.experimental.pallas import tpu as pltpu
from jax.sharding import PartitionSpec as P

MESH = pl.DeviceIdType.MESH


def split_chunks(depth, most):
    count = most
    while depth % count:
        count -= 1
    return count


def kernel(
    sizes,
    momentum_in,
    directions_in,
    v_ref,
    links_ref,
    links_far,
    out_ref,
    ext,
    left,
    rim_y,
    rim_z,
    tab_x,
    tab_y,
    tab_z,
    cos_ref,
    sin_ref,
    trans,
    acc,
    momentum_ref,
    directions_ref,
    outgo,
    income,
    reduced,
    gathered,
    local_sem,
    send_sem,
    recv_sem,
    red_sem,
):
    gz_n, gy_n, vec_n, depth, height, rows, width, chunks = sizes
    pairs = vec_n // 2
    lanes = 2 * width
    me_z = lax.axis_index("gz")
    me_y = lax.axis_index("gy")
    me_v = lax.axis_index("vec")
    pair = me_v // 2
    side = lax.rem(me_v, 2)
    group = gz_n * gy_n
    me_g = me_z * gy_n + me_y
    span = depth // chunks

    def member(step):
        return lax.rem(me_g + step, group)

    def place(g):
        return {"gz": g // gy_n, "gy": lax.rem(g, gy_n)}

    barrier = pltpu.get_barrier_semaphore()
    for step in range(1, group):
        pl.semaphore_signal(barrier, inc=1, device_id=place(member(step)), device_id_type=MESH)
    for step in range(1, vec_n):
        pl.semaphore_signal(
            barrier, inc=1, device_id={"vec": lax.rem(me_v + step, vec_n)}, device_id_type=MESH
        )
    centre = ext.at[pl.ds(1, depth), pl.ds(1, height)]
    locals_ = [
        pltpu.make_async_copy(v_ref, centre, local_sem.at[0]),
        pltpu.make_async_copy(v_ref, left.at[pair, side], local_sem.at[1]),
    ]
    scalars = [
        pltpu.make_async_copy(momentum_in, momentum_ref, local_sem.at[2]),
        pltpu.make_async_copy(directions_in, directions_ref, local_sem.at[3]),
    ]
    for copy in scalars + locals_:
        copy.start()
    pl.semaphore_wait(barrier, group - 1 + vec_n - 1)

    counter = [0]

    def remote(src, dst, device):
        index = counter[0]
        counter[0] += 1
        return pltpu.make_async_remote_copy(
            src_ref=src,
            dst_ref=dst,
            send_sem=send_sem.at[index],
            recv_sem=recv_sem.at[index],
            device_id=device,
            device_id_type=MESH,
        )

    z_up = {"gz": lax.rem(me_z + 1, gz_n)}
    z_down = {"gz": lax.rem(me_z + gz_n - 1, gz_n)}
    y_up = {"gy": lax.rem(me_y + 1, gy_n)}
    y_down = {"gy": lax.rem(me_y + gy_n - 1, gy_n)}
    sibling = {"vec": pair * 2 + 1 - side}
    inner_y = pl.ds(1, height)
    z_copies = [
        remote(v_ref.at[depth - 1], ext.at[0, inner_y], z_up),
        remote(v_ref.at[0], ext.at[depth + 1, inner_y], z_down),
        remote(links_far.at[2, depth - 1], rim_z, z_up),
    ]
    rim_copy = remote(links_far.at[1, :, height - 1], rim_y, y_up)
    near = remote(v_ref, left.at[pair, side], sibling)
    far, relay, y_copies = [], [], []
    for k in range(chunks):
        part = pl.ds(k * span, span)
        inner_z = pl.ds(1 + k * span, span)
        y_copies.append(
            (
                remote(v_ref.at[part, height - 1], ext.at[inner_z, 0], y_up),
                remote(v_ref.at[part, 0], ext.at[inner_z, height + 1], y_down),
            )
        )
        for hop in range(1, pairs):
            target = lax.rem(pair + hop, pairs)
            source = lax.rem(pair + pairs - hop, pairs)
            far.append(
                remote(v_ref.at[part], left.at[pair, side, part], {"vec": target * 2 + side})
            )
            relay.append(
                remote(left.at[source, side, part], left.at[source, side, part], sibling)
            )
    rim_copy.start()
    for copy in z_copies:
        copy.start()
    for k in range(chunks):
        for copy in far[k * (pairs - 1) : (k + 1) * (pairs - 1)]:
            copy.start()
        for copy in y_copies[k]:
            copy.start()
    near.start()

    lane = lax.broadcasted_iota(jnp.int32, (1, lanes), 1)
    low_half = lane < width
    last_mask = lax.rem(lane, width) == width - 1
    first_mask = lax.rem(lane, width) == 0
    sign = jnp.where(low_half, 1.0, -1.0).astype(jnp.float32)
    tile = 32 if rows % 32 == 0 else rows

    for copy in scalars:
        copy.wait()
    site_shape = (depth * height, lanes)
    site = lax.broadcasted_iota(jnp.int32, site_shape, 0)
    x_at = lax.rem(lax.broadcasted_iota(jnp.int32, site_shape, 1), width)
    y_at = me_y * height + lax.rem(site, height)
    z_at = me_z * depth + site // height

    def fraction(component, at, extent):
        turned = lax.rem(momentum_ref[component] * at, extent)
        turned = jnp.where(turned < 0, turned + extent, turned)
        return turned.astype(jnp.float32) / extent

    angle = (2.0 * math.pi) * (
        fraction(2, z_at, depth * gz_n)
        + fraction(1, y_at, height * gy_n)
        + fraction(0, x_at, width)
    )
    cos_ref[...] = jnp.cos(angle)
    sin_ref[...] = jnp.sin(angle) * sign

    def coefficients(raw):
        value = raw.astype(jnp.float32) * 0.5
        swapped = pltpu.roll(value, width, 1)
        real = jnp.where(low_half, value, swapped)
        imag = jnp.where(low_half, -swapped, value)
        return real, imag

    def put(table, where, pair_of):
        table[where + (slice(0, 9),)] = pair_of[0]
        table[where + (slice(16, 25),)] = pair_of[1]

    def step_back(value):
        one = pltpu.roll(value, 1, 1)
        two = pltpu.roll(value, width + 1, 1)
        return jnp.where(first_mask, two, one)

    def make_tables(z):
        for y in range(height):
            real, imag = coefficients(links_ref[0, z, y])
            put(tab_x, (0, z, y), (real, imag))
            put(tab_x, (1, z, y), (step_back(real), step_back(imag)))
            put(tab_y, (z, y + 1), coefficients(links_ref[1, z, y]))
            put(tab_z, (z + 1, y), coefficients(links_ref[2, z, y]))

    pl.loop(0, depth)(make_tables)

    def store(z, y, colour, slot, lo, value):
        turned = pltpu.roll(value, width, 1) * sign
        trans[z, y, colour, pl.ds(slot * 2 * rows + lo, tile)] = value.astype(jnp.bfloat16)
        trans[z, y, colour, pl.ds((slot * 2 + 1) * rows + lo, tile)] = turned.astype(jnp.bfloat16)

    def load(z, y, colour, lo):
        return ext[z, y, colour, pl.ds(lo, tile)].astype(jnp.float32)

    def stencil(z, y, lo, slot, ahead, behind, up, down):
        sums = [0.0, 0.0, 0.0]
        for col in range(3):
            value, swapped = ahead(col)
            for row in range(3):
                k = row * 3 + col
                sums[row] = sums[row] + (up(k) * value + up(16 + k) * swapped)
        for col in range(3):
            value, swapped = behind(col)
            for row in range(3):
                k = col * 3 + row
                sums[row] = sums[row] + (down(16 + k) * swapped - down(k) * value)
        for row in range(3):
            store(z, y, row, slot, lo, sums[row])

    def swap(value):
        return value, pltpu.roll(value, width, 1)

    def pass_x(z):
        for y in range(height):
            for lo in range(0, rows, tile):
                here = pl.ds(z * height + y, 1)
                cosine = cos_ref[here]
                sine = sin_ref[here]

                def ahead(col):
                    value = load(z + 1, y + 1, col, lo)
                    one = pltpu.roll(value, lanes - 1, 1)
                    two = pltpu.roll(value, width - 1, 1)
                    return jnp.where(last_mask, two, one), jnp.where(last_mask, one, two)

                def behind(col):
                    value = load(z + 1, y + 1, col, lo)
                    one = pltpu.roll(value, 1, 1)
                    two = pltpu.roll(value, width + 1, 1)
                    return jnp.where(first_mask, two, one), jnp.where(first_mask, one, two)

                stencil(
                    z, y, lo, 0, ahead, behind,
                    lambda k: tab_x[0, z, y, k : k + 1],
                    lambda k: tab_x[1, z, y, k : k + 1],
                )
                for col in range(3):
                    value, swapped = swap(load(z + 1, y + 1, col, lo))
                    store(z, y, col, 2, lo, value * cosine + swapped * sine)

    def pass_y(z):
        for y in range(height):
            for lo in range(0, rows, tile):
                stencil(
                    z, y, lo, 3,
                    lambda col: swap(load(z + 1, y + 2, col, lo)),
                    lambda col: swap(load(z + 1, y, col, lo)),
                    lambda k: tab_y[z, y + 1, k : k + 1],
                    lambda k: tab_y[z, y, k : k + 1],
                )

    def pass_z(z):
        for y in range(height):
            for lo in range(0, rows, tile):
                stencil(
                    z, y, lo, 1,
                    lambda col: swap(load(z + 2, y + 1, col, lo)),
                    lambda col: swap(load(z, y + 1, col, lo)),
                    lambda k: tab_z[z + 1, y, k : k + 1],
                    lambda k: tab_z[z, y, k : k + 1],
                )

    def contract(which, chunk, lo, hi, fresh):
        sites = [
            (chunk * span + dz, y, c) for dz in range(span) for y in range(height) for c in range(3)
        ]
        a = jnp.concatenate([trans[z, y, c, lo:hi] for z, y, c in sites], axis=1)
        b = jnp.concatenate(
            [
                jnp.concatenate([left[which, s, z, y, c] for z, y, c in sites], axis=1)
                for s in range(2)
            ],
            axis=0,
        )
        product = lax.dot_general(
            a, b, (((1,), (1,)), ((), ())), preferred_element_type=jnp.float32
        )
        columns = pl.ds(pl.multiple_of(which * 2 * rows, 2 * rows), 2 * rows)
        if fresh:
            acc[lo:hi, columns] = product
        else:
            acc[lo:hi, columns] += product

    for copy in locals_:
        copy.wait()
    pl.loop(0, depth)(pass_x)
    for copy in z_copies:
        copy.wait()
    for y in range(height):
        put(tab_z, (0, y), coefficients(rim_z[y]))
    pl.loop(0, depth)(pass_z)

    early = 6 * rows
    near.wait()
    contract(pair, 0, 0, early, True)
    pl.loop(1, chunks)(lambda k: contract(pair, k, 0, early, False))

    own_columns = pl.ds(pl.multiple_of(pair * 2 * rows, 2 * rows), 2 * rows)
    stages = [
        [(own_columns, 0, early)],
        [
            (
                pl.ds(
                    pl.multiple_of(lax.rem(pair + pairs - hop, pairs) * 2 * rows, 2 * rows),
                    2 * rows,
                ),
                0,
                8 * rows,
            )
            for hop in range(1, pairs)
        ]
        + [(own_columns, early, 8 * rows)],
    ]

    def exchange(stage, phase, step):
        source = outgo[stage].at[member(step)] if phase == 0 else reduced[stage]
        target = income[stage] if phase == 0 else gathered[stage]
        return pltpu.make_async_remote_copy(
            src_ref=source,
            dst_ref=target.at[me_g],
            send_sem=red_sem.at[stage, phase, 0, step],
            recv_sem=red_sem.at[stage, phase, 1, step],
            device_id=place(member(step)),
            device_id_type=MESH,
        )

    def pieces(stage):
        at = 0
        for columns, lo, hi in stages[stage]:
            share = (hi - lo) // group
            yield columns, lo, share, at
            at += share

    def scatter_start(stage):
        for columns, lo, share, at in pieces(stage):
            for g in range(group):
                outgo[stage][g, at : at + share] = acc[
                    lo + g * share : lo + (g + 1) * share, columns
                ].astype(jnp.bfloat16)
        for step in range(1, group):
            exchange(stage, 0, step).start()

    def gather_start(stage):
        for step in range(1, group):
            exchange(stage, 0, step).wait()
        total = outgo[stage][me_g].astype(jnp.float32)
        for step in range(1, group):
            total = total + income[stage][member(step)].astype(jnp.float32)
        reduced[stage][...] = total.astype(jnp.bfloat16)
        gathered[stage][me_g] = total.astype(jnp.bfloat16)
        for step in range(1, group):
            exchange(stage, 1, step).start()

    def gather_finish(stage):
        for step in range(1, group):
            exchange(stage, 1, step).wait()
        for columns, lo, share, at in pieces(stage):
            for g in range(group):
                acc[lo + g * share : lo + (g + 1) * share, columns] = gathered[stage][
                    g, at : at + share
                ].astype(jnp.float32)

    scatter_start(0)
    rim_copy.wait()

    @pl.loop(0, depth)
    def _(z):
        put(tab_y, (z, 0), coefficients(rim_y[z]))

    for k in range(chunks + 1):
        if k < chunks:
            for copy in y_copies[k]:
                copy.wait()
            pl.loop(k * span, (k + 1) * span)(pass_y)
            contract(pair, k, early, 8 * rows, k == 0)
            for hop in range(1, pairs):
                index = k * (pairs - 1) + hop - 1
                far[index].wait()
                relay[index].start()
        if k == chunks - 1:
            gather_start(0)
        if k:
            for hop in range(1, pairs):
                relay[(k - 1) * (pairs - 1) + hop - 1].wait()
                contract(lax.rem(pair + pairs - hop, pairs), k - 1, 0, 8 * rows, k == 1)

    scatter_start(1)
    gather_start(1)
    gather_finish(0)
    gather_finish(1)

    scale = 1.0 / math.sqrt(width * height * gy_n * depth * gz_n)
    full = acc[...] * scale
    along_x, along_z, phased, along_y = [
        full[slot * 2 * rows : (slot + 1) * 2 * rows] for slot in range(4)
    ]
    for slot in range(3):
        chosen = directions_ref[slot]
        out_ref[slot * 2 * rows : (slot + 1) * 2 * rows] = jnp.where(
            chosen == 0, along_x, jnp.where(chosen == 1, along_y, along_z)
        )
    out_ref[6 * rows :] = phased


def body(vectors, links, momentum, directions):
    rows, _, depth, height, lanes = vectors.shape
    gz_n = lax.axis_size("gz")
    gy_n = lax.axis_size("gy")
    vec_n = lax.axis_size("vec")
    group = gz_n * gy_n
    chunks = split_chunks(depth, 4)
    v = jnp.transpose(vectors, (2, 3, 1, 0, 4))
    packed = jnp.transpose(links, (0, 3, 4, 1, 2, 5)).reshape(3, depth, height, 9, lanes)

    bf16, f32 = jnp.bfloat16, jnp.float32
    pairs = vec_n // 2
    shares = (6 * rows // group, (8 * (pairs - 1) + 2) * rows // group)
    remote_count = 5 + chunks * (2 + 2 * (pairs - 1))
    vmem = pl.BlockSpec(memory_space=pltpu.VMEM)
    hbm = pl.BlockSpec(memory_space=pl.ANY)
    sizes = (gz_n, gy_n, vec_n, depth, height, rows, lanes // 2, chunks)
    out = pl.pallas_call(
        functools.partial(kernel, sizes),
        out_shape=jax.ShapeDtypeStruct((8 * rows, vec_n * rows), f32),
        in_specs=[hbm, hbm, hbm, vmem, hbm],
        out_specs=vmem,
        scratch_shapes=[
            pltpu.VMEM((depth + 2, height + 2, 3, rows, lanes), bf16),
            pltpu.VMEM((pairs, 2, depth, height, 3, rows, lanes), bf16),
            pltpu.VMEM((depth, 9, lanes), bf16),
            pltpu.VMEM((height, 9, lanes), bf16),
            pltpu.VMEM((2, depth, height, 32, lanes), f32),
            pltpu.VMEM((depth, height + 1, 32, lanes), f32),
            pltpu.VMEM((depth + 1, height, 32, lanes), f32),
            pltpu.VMEM((depth * height, lanes), f32),
            pltpu.VMEM((depth * height, lanes), f32),
            pltpu.VMEM((depth, height, 3, 8 * rows, lanes), bf16),
            pltpu.VMEM((8 * rows, vec_n * rows), f32),
            pltpu.SMEM((3,), jnp.int32),
            pltpu.SMEM((3,), jnp.int32),
            [pltpu.VMEM((group, share, 2 * rows), bf16) for share in shares],
            [pltpu.VMEM((group, share, 2 * rows), bf16) for share in shares],
            [pltpu.VMEM((share, 2 * rows), bf16) for share in shares],
            [pltpu.VMEM((group, share, 2 * rows), bf16) for share in shares],
            pltpu.SemaphoreType.DMA((4,)),
            pltpu.SemaphoreType.DMA((remote_count,)),
            pltpu.SemaphoreType.DMA((remote_count,)),
            pltpu.SemaphoreType.DMA((2, 2, 2, group)),
        ],
        compiler_params=pltpu.CompilerParams(
            collective_id=0, has_side_effects=True, vmem_limit_bytes=48 * 1024 * 1024
        ),
    )(momentum, directions, v, packed, packed)
    return out.reshape(4, 2, rows, vec_n * rows)


def solution(mesh):
    in_specs = (P("vec", None, "gz", "gy", None), P(None, None, None, "gz", "gy", None), P(), P())
    out_specs = P(None, None, "vec", None)
    return jax.shard_map(body, mesh=mesh, in_specs=in_specs, out_specs=out_specs, check_vma=False)
```

```python
import functools
import math

import jax
import jax.numpy as jnp
from jax import lax
from jax.experimental import pallas as pl
from jax.experimental.pallas import tpu as pltpu
from jax.sharding import PartitionSpec as P

MESH = pl.DeviceIdType.MESH


def split_chunks(depth, most):
    count = most
    while depth % count:
        count -= 1
    return count


def kernel(
    sizes,
    momentum_in,
    directions_in,
    v_ref,
    links_ref,
    links_far,
    out_ref,
    ext,
    left,
    rim_y,
    rim_z,
    tab_x,
    tab_y,
    tab_z,
    cos_ref,
    sin_ref,
    trans,
    acc,
    momentum_ref,
    directions_ref,
    outgo,
    income,
    reduced,
    gathered,
    local_sem,
    send_sem,
    recv_sem,
    red_sem,
):
    gz_n, gy_n, vec_n, depth, height, rows, width, chunks = sizes
    pairs = vec_n // 2
    lanes = 2 * width
    me_z = lax.axis_index("gz")
    me_y = lax.axis_index("gy")
    me_v = lax.axis_index("vec")
    pair = me_v // 2
    side = lax.rem(me_v, 2)
    group = gz_n * gy_n
    me_g = me_z * gy_n + me_y
    span = depth // chunks

    def member(step):
        return lax.rem(me_g + step, group)

    def place(g):
        return {"gz": g // gy_n, "gy": lax.rem(g, gy_n)}

    barrier = pltpu.get_barrier_semaphore()
    for step in range(1, group):
        pl.semaphore_signal(barrier, inc=1, device_id=place(member(step)), device_id_type=MESH)
    for step in range(1, vec_n):
        pl.semaphore_signal(
            barrier, inc=1, device_id={"vec": lax.rem(me_v + step, vec_n)}, device_id_type=MESH
        )
    centre = ext.at[pl.ds(1, depth), pl.ds(1, height)]
    locals_ = [
        pltpu.make_async_copy(v_ref, centre, local_sem.at[0]),
        pltpu.make_async_copy(v_ref, left.at[pair, side], local_sem.at[1]),
    ]
    scalars = [
        pltpu.make_async_copy(momentum_in, momentum_ref, local_sem.at[2]),
        pltpu.make_async_copy(directions_in, directions_ref, local_sem.at[3]),
    ]
    for copy in scalars + locals_:
        copy.start()
    pl.semaphore_wait(barrier, group - 1 + vec_n - 1)

    counter = [0]

    def remote(src, dst, device):
        index = counter[0]
        counter[0] += 1
        return pltpu.make_async_remote_copy(
            src_ref=src,
            dst_ref=dst,
            send_sem=send_sem.at[index],
            recv_sem=recv_sem.at[index],
            device_id=device,
            device_id_type=MESH,
        )

    z_up = {"gz": lax.rem(me_z + 1, gz_n)}
    z_down = {"gz": lax.rem(me_z + gz_n - 1, gz_n)}
    y_up = {"gy": lax.rem(me_y + 1, gy_n)}
    y_down = {"gy": lax.rem(me_y + gy_n - 1, gy_n)}
    sibling = {"vec": pair * 2 + 1 - side}
    inner_y = pl.ds(1, height)
    z_copies = [
        remote(v_ref.at[depth - 1], ext.at[0, inner_y], z_up),
        remote(v_ref.at[0], ext.at[depth + 1, inner_y], z_down),
        remote(links_far.at[2, depth - 1], rim_z, z_up),
    ]
    rim_copy = remote(links_far.at[1, :, height - 1], rim_y, y_up)
    near = remote(v_ref, left.at[pair, side], sibling)
    far, relay, y_copies = [], [], []
    for k in range(chunks):
        part = pl.ds(k * span, span)
        inner_z = pl.ds(1 + k * span, span)
        y_copies.append(
            (
                remote(v_ref.at[part, height - 1], ext.at[inner_z, 0], y_up),
                remote(v_ref.at[part, 0], ext.at[inner_z, height + 1], y_down),
            )
        )
        for hop in range(1, pairs):
            target = lax.rem(pair + hop, pairs)
            source = lax.rem(pair + pairs - hop, pairs)
            far.append(
                remote(v_ref.at[part], left.at[pair, side, part], {"vec": target * 2 + side})
            )
            relay.append(
                remote(left.at[source, side, part], left.at[source, side, part], sibling)
            )
    rim_copy.start()
    for copy in z_copies:
        copy.start()
    for k in range(chunks):
        for copy in far[k * (pairs - 1) : (k + 1) * (pairs - 1)]:
            copy.start()
        for copy in y_copies[k]:
            copy.start()
    near.start()

    lane = lax.broadcasted_iota(jnp.int32, (1, lanes), 1)
    low_half = lane < width
    last_mask = lax.rem(lane, width) == width - 1
    first_mask = lax.rem(lane, width) == 0
    sign = jnp.where(low_half, 1.0, -1.0).astype(jnp.float32)
    tile = 32 if rows % 32 == 0 else rows

    for copy in scalars:
        copy.wait()
    site_shape = (depth * height, lanes)
    site = lax.broadcasted_iota(jnp.int32, site_shape, 0)
    x_at = lax.rem(lax.broadcasted_iota(jnp.int32, site_shape, 1), width)
    y_at = me_y * height + lax.rem(site, height)
    z_at = me_z * depth + site // height

    def fraction(component, at, extent):
        turned = lax.rem(momentum_ref[component] * at, extent)
        turned = jnp.where(turned < 0, turned + extent, turned)
        return turned.astype(jnp.float32) / extent

    angle = (2.0 * math.pi) * (
        fraction(2, z_at, depth * gz_n)
        + fraction(1, y_at, height * gy_n)
        + fraction(0, x_at, width)
    )
    cos_ref[...] = jnp.cos(angle)
    sin_ref[...] = jnp.sin(angle) * sign

    def coefficients(raw):
        value = raw.astype(jnp.float32) * 0.5
        swapped = pltpu.roll(value, width, 1)
        real = jnp.where(low_half, value, swapped)
        imag = jnp.where(low_half, -swapped, value)
        return real, imag

    def put(table, where, pair_of):
        table[where + (slice(0, 9),)] = pair_of[0]
        table[where + (slice(16, 25),)] = pair_of[1]

    def step_back(value):
        one = pltpu.roll(value, 1, 1)
        two = pltpu.roll(value, width + 1, 1)
        return jnp.where(first_mask, two, one)

    def make_tables(z):
        for y in range(height):
            real, imag = coefficients(links_ref[0, z, y])
            put(tab_x, (0, z, y), (real, imag))
            put(tab_x, (1, z, y), (step_back(real), step_back(imag)))
            put(tab_y, (z, y + 1), coefficients(links_ref[1, z, y]))
            put(tab_z, (z + 1, y), coefficients(links_ref[2, z, y]))

    pl.loop(0, depth)(make_tables)

    def store(z, y, colour, slot, lo, value):
        turned = pltpu.roll(value, width, 1) * sign
        trans[z, y, colour, pl.ds(slot * 2 * rows + lo, tile)] = value.astype(jnp.bfloat16)
        trans[z, y, colour, pl.ds((slot * 2 + 1) * rows + lo, tile)] = turned.astype(jnp.bfloat16)

    def load(z, y, colour, lo):
        return ext[z, y, colour, pl.ds(lo, tile)].astype(jnp.float32)

    def stencil(z, y, lo, slot, ahead, behind, up, down):
        sums = [0.0, 0.0, 0.0]
        for col in range(3):
            value, swapped = ahead(col)
            for row in range(3):
                k = row * 3 + col
                sums[row] = sums[row] + (up(k) * value + up(16 + k) * swapped)
        for col in range(3):
            value, swapped = behind(col)
            for row in range(3):
                k = col * 3 + row
                sums[row] = sums[row] + (down(16 + k) * swapped - down(k) * value)
        for row in range(3):
            store(z, y, row, slot, lo, sums[row])

    def swap(value):
        return value, pltpu.roll(value, width, 1)

    def pass_x(z):
        for y in range(height):
            for lo in range(0, rows, tile):
                here = pl.ds(z * height + y, 1)
                cosine = cos_ref[here]
                sine = sin_ref[here]

                def ahead(col):
                    value = load(z + 1, y + 1, col, lo)
                    one = pltpu.roll(value, lanes - 1, 1)
                    two = pltpu.roll(value, width - 1, 1)
                    return jnp.where(last_mask, two, one), jnp.where(last_mask, one, two)

                def behind(col):
                    value = load(z + 1, y + 1, col, lo)
                    one = pltpu.roll(value, 1, 1)
                    two = pltpu.roll(value, width + 1, 1)
                    return jnp.where(first_mask, two, one), jnp.where(first_mask, one, two)

                stencil(
                    z, y, lo, 0, ahead, behind,
                    lambda k: tab_x[0, z, y, k : k + 1],
                    lambda k: tab_x[1, z, y, k : k + 1],
                )
                for col in range(3):
                    value, swapped = swap(load(z + 1, y + 1, col, lo))
                    store(z, y, col, 2, lo, value * cosine + swapped * sine)

    def pass_y(z):
        for y in range(height):
            for lo in range(0, rows, tile):
                stencil(
                    z, y, lo, 3,
                    lambda col: swap(load(z + 1, y + 2, col, lo)),
                    lambda col: swap(load(z + 1, y, col, lo)),
                    lambda k: tab_y[z, y + 1, k : k + 1],
                    lambda k: tab_y[z, y, k : k + 1],
                )

    def pass_z(z):
        for y in range(height):
            for lo in range(0, rows, tile):
                stencil(
                    z, y, lo, 1,
                    lambda col: swap(load(z + 2, y + 1, col, lo)),
                    lambda col: swap(load(z, y + 1, col, lo)),
                    lambda k: tab_z[z + 1, y, k : k + 1],
                    lambda k: tab_z[z, y, k : k + 1],
                )

    def contract(which, chunk, lo, hi, fresh):
        sites = [
            (chunk * span + dz, y, c) for dz in range(span) for y in range(height) for c in range(3)
        ]
        a = jnp.concatenate([trans[z, y, c, lo:hi] for z, y, c in sites], axis=1)
        b = jnp.concatenate(
            [
                jnp.concatenate([left[which, s, z, y, c] for z, y, c in sites], axis=1)
                for s in range(2)
            ],
            axis=0,
        )
        product = lax.dot_general(
            a, b, (((1,), (1,)), ((), ())), preferred_element_type=jnp.float32
        )
        columns = pl.ds(pl.multiple_of(which * 2 * rows, 2 * rows), 2 * rows)
        if fresh:
            acc[lo:hi, columns] = product
        else:
            acc[lo:hi, columns] += product

    for copy in locals_:
        copy.wait()
    pl.loop(0, depth)(pass_x)
    for copy in z_copies:
        copy.wait()
    for y in range(height):
        put(tab_z, (0, y), coefficients(rim_z[y]))
    pl.loop(0, depth)(pass_z)

    early = 6 * rows
    near.wait()
    contract(pair, 0, 0, early, True)
    pl.loop(1, chunks)(lambda k: contract(pair, k, 0, early, False))

    own_columns = pl.ds(pl.multiple_of(pair * 2 * rows, 2 * rows), 2 * rows)
    stages = [
        [(own_columns, 0, early)],
        [
            (
                pl.ds(
                    pl.multiple_of(lax.rem(pair + pairs - hop, pairs) * 2 * rows, 2 * rows),
                    2 * rows,
                ),
                0,
                8 * rows,
            )
            for hop in range(1, pairs)
        ]
        + [(own_columns, early, 8 * rows)],
    ]

    def exchange(stage, phase, step):
        source = outgo[stage].at[member(step)] if phase == 0 else reduced[stage]
        target = income[stage] if phase == 0 else gathered[stage]
        return pltpu.make_async_remote_copy(
            src_ref=source,
            dst_ref=target.at[me_g],
            send_sem=red_sem.at[stage, phase, 0, step],
            recv_sem=red_sem.at[stage, phase, 1, step],
            device_id=place(member(step)),
            device_id_type=MESH,
        )

    def pieces(stage):
        at = 0
        for columns, lo, hi in stages[stage]:
            share = (hi - lo) // group
            yield columns, lo, share, at
            at += share

    def scatter_start(stage):
        for columns, lo, share, at in pieces(stage):
            for g in range(group):
                outgo[stage][g, at : at + share] = acc[
                    lo + g * share : lo + (g + 1) * share, columns
                ].astype(jnp.bfloat16)
        for step in range(1, group):
            exchange(stage, 0, step).start()

    def gather_start(stage):
        for step in range(1, group):
            exchange(stage, 0, step).wait()
        total = outgo[stage][me_g].astype(jnp.float32)
        for step in range(1, group):
            total = total + income[stage][member(step)].astype(jnp.float32)
        reduced[stage][...] = total.astype(jnp.bfloat16)
        gathered[stage][me_g] = total.astype(jnp.bfloat16)
        for step in range(1, group):
            exchange(stage, 1, step).start()

    def gather_finish(stage):
        for step in range(1, group):
            exchange(stage, 1, step).wait()
        for columns, lo, share, at in pieces(stage):
            for g in range(group):
                acc[lo + g * share : lo + (g + 1) * share, columns] = gathered[stage][
                    g, at : at + share
                ].astype(jnp.float32)

    scatter_start(0)
    rim_copy.wait()

    @pl.loop(0, depth)
    def _(z):
        put(tab_y, (z, 0), coefficients(rim_y[z]))

    for k in range(chunks + 1):
        if k < chunks:
            for hop in range(1, pairs):
                index = k * (pairs - 1) + hop - 1
                far[index].wait()
                relay[index].start()
            for copy in y_copies[k]:
                copy.wait()
            pl.loop(k * span, (k + 1) * span)(pass_y)
            contract(pair, k, early, 8 * rows, k == 0)
        if k == chunks - 1:
            gather_start(0)
        if k:
            for hop in range(1, pairs):
                relay[(k - 1) * (pairs - 1) + hop - 1].wait()
                contract(lax.rem(pair + pairs - hop, pairs), k - 1, 0, 8 * rows, k == 1)

    scatter_start(1)
    gather_start(1)
    gather_finish(0)
    gather_finish(1)

    scale = 1.0 / math.sqrt(width * height * gy_n * depth * gz_n)
    full = acc[...] * scale
    along_x, along_z, phased, along_y = [
        full[slot * 2 * rows : (slot + 1) * 2 * rows] for slot in range(4)
    ]
    for slot in range(3):
        chosen = directions_ref[slot]
        out_ref[slot * 2 * rows : (slot + 1) * 2 * rows] = jnp.where(
            chosen == 0, along_x, jnp.where(chosen == 1, along_y, along_z)
        )
    out_ref[6 * rows :] = phased


def body(vectors, links, momentum, directions):
    rows, _, depth, height, lanes = vectors.shape
    gz_n = lax.axis_size("gz")
    gy_n = lax.axis_size("gy")
    vec_n = lax.axis_size("vec")
    group = gz_n * gy_n
    chunks = split_chunks(depth, 8)
    v = jnp.transpose(vectors, (2, 3, 1, 0, 4))
    packed = jnp.transpose(links, (0, 3, 4, 1, 2, 5)).reshape(3, depth, height, 9, lanes)

    bf16, f32 = jnp.bfloat16, jnp.float32
    pairs = vec_n // 2
    shares = (6 * rows // group, (8 * (pairs - 1) + 2) * rows // group)
    remote_count = 5 + chunks * (2 + 2 * (pairs - 1))
    vmem = pl.BlockSpec(memory_space=pltpu.VMEM)
    hbm = pl.BlockSpec(memory_space=pl.ANY)
    sizes = (gz_n, gy_n, vec_n, depth, height, rows, lanes // 2, chunks)
    out = pl.pallas_call(
        functools.partial(kernel, sizes),
        out_shape=jax.ShapeDtypeStruct((8 * rows, vec_n * rows), f32),
        in_specs=[hbm, hbm, hbm, vmem, hbm],
        out_specs=vmem,
        scratch_shapes=[
            pltpu.VMEM((depth + 2, height + 2, 3, rows, lanes), bf16),
            pltpu.VMEM((pairs, 2, depth, height, 3, rows, lanes), bf16),
            pltpu.VMEM((depth, 9, lanes), bf16),
            pltpu.VMEM((height, 9, lanes), bf16),
            pltpu.VMEM((2, depth, height, 32, lanes), f32),
            pltpu.VMEM((depth, height + 1, 32, lanes), f32),
            pltpu.VMEM((depth + 1, height, 32, lanes), f32),
            pltpu.VMEM((depth * height, lanes), f32),
            pltpu.VMEM((depth * height, lanes), f32),
            pltpu.VMEM((depth, height, 3, 8 * rows, lanes), bf16),
            pltpu.VMEM((8 * rows, vec_n * rows), f32),
            pltpu.SMEM((3,), jnp.int32),
            pltpu.SMEM((3,), jnp.int32),
            [pltpu.VMEM((group, share, 2 * rows), bf16) for share in shares],
            [pltpu.VMEM((group, share, 2 * rows), bf16) for share in shares],
            [pltpu.VMEM((share, 2 * rows), bf16) for share in shares],
            [pltpu.VMEM((group, share, 2 * rows), bf16) for share in shares],
            pltpu.SemaphoreType.DMA((4,)),
            pltpu.SemaphoreType.DMA((remote_count,)),
            pltpu.SemaphoreType.DMA((remote_count,)),
            pltpu.SemaphoreType.DMA((2, 2, 2, group)),
        ],
        compiler_params=pltpu.CompilerParams(
            collective_id=0, has_side_effects=True, vmem_limit_bytes=48 * 1024 * 1024
        ),
    )(momentum, directions, v, packed, packed)
    return out.reshape(4, 2, rows, vec_n * rows)


def solution(mesh):
    in_specs = (P("vec", None, "gz", "gy", None), P(None, None, None, "gz", "gy", None), P(), P())
    out_specs = P(None, None, "vec", None)
    return jax.shard_map(body, mesh=mesh, in_specs=in_specs, out_specs=out_specs, check_vma=False)
```

```python
import functools
import math

import jax
import jax.numpy as jnp
from jax import lax
from jax.experimental import pallas as pl
from jax.experimental.pallas import tpu as pltpu
from jax.sharding import PartitionSpec as P

MESH = pl.DeviceIdType.MESH


def split_chunks(depth, most):
    count = most
    while depth % count:
        count -= 1
    return count


def kernel(
    sizes,
    momentum_in,
    directions_in,
    v_ref,
    links_ref,
    links_far,
    out_ref,
    ext,
    left,
    rim_y,
    rim_z,
    tab_x,
    tab_y,
    tab_z,
    cos_ref,
    sin_ref,
    trans,
    acc,
    momentum_ref,
    directions_ref,
    outgo,
    income,
    reduced,
    gathered,
    local_sem,
    send_sem,
    recv_sem,
    red_sem,
):
    gz_n, gy_n, vec_n, depth, height, rows, width, chunks = sizes
    pairs = vec_n // 2
    lanes = 2 * width
    me_z = lax.axis_index("gz")
    me_y = lax.axis_index("gy")
    me_v = lax.axis_index("vec")
    pair = me_v // 2
    side = lax.rem(me_v, 2)
    group = gz_n * gy_n
    me_g = me_z * gy_n + me_y
    span = depth // chunks

    def member(step):
        return lax.rem(me_g + step, group)

    def place(g):
        return {"gz": g // gy_n, "gy": lax.rem(g, gy_n)}

    barrier = pltpu.get_barrier_semaphore()
    for step in range(1, group):
        pl.semaphore_signal(barrier, inc=1, device_id=place(member(step)), device_id_type=MESH)
    for step in range(1, vec_n):
        pl.semaphore_signal(
            barrier, inc=1, device_id={"vec": lax.rem(me_v + step, vec_n)}, device_id_type=MESH
        )
    centre = ext.at[pl.ds(1, depth), pl.ds(1, height)]
    locals_ = [
        pltpu.make_async_copy(v_ref, centre, local_sem.at[0]),
        pltpu.make_async_copy(v_ref, left.at[pair, side], local_sem.at[1]),
    ]
    scalars = [
        pltpu.make_async_copy(momentum_in, momentum_ref, local_sem.at[2]),
        pltpu.make_async_copy(directions_in, directions_ref, local_sem.at[3]),
    ]
    for copy in scalars + locals_:
        copy.start()
    pl.semaphore_wait(barrier, group - 1 + vec_n - 1)

    counter = [0]

    def remote(src, dst, device):
        index = counter[0]
        counter[0] += 1
        return pltpu.make_async_remote_copy(
            src_ref=src,
            dst_ref=dst,
            send_sem=send_sem.at[index],
            recv_sem=recv_sem.at[index],
            device_id=device,
            device_id_type=MESH,
        )

    z_up = {"gz": lax.rem(me_z + 1, gz_n)}
    z_down = {"gz": lax.rem(me_z + gz_n - 1, gz_n)}
    y_up = {"gy": lax.rem(me_y + 1, gy_n)}
    y_down = {"gy": lax.rem(me_y + gy_n - 1, gy_n)}
    sibling = {"vec": pair * 2 + 1 - side}
    inner_y = pl.ds(1, height)
    z_copies = [
        remote(v_ref.at[depth - 1], ext.at[0, inner_y], z_up),
        remote(v_ref.at[0], ext.at[depth + 1, inner_y], z_down),
        remote(links_far.at[2, depth - 1], rim_z, z_up),
    ]
    rim_copy = remote(links_far.at[1, :, height - 1], rim_y, y_up)
    near = remote(v_ref, left.at[pair, side], sibling)
    far, relay, y_copies = [], [], []
    for k in range(chunks):
        part = pl.ds(k * span, span)
        inner_z = pl.ds(1 + k * span, span)
        y_copies.append(
            (
                remote(v_ref.at[part, height - 1], ext.at[inner_z, 0], y_up),
                remote(v_ref.at[part, 0], ext.at[inner_z, height + 1], y_down),
            )
        )
        for hop in range(1, pairs):
            target = lax.rem(pair + hop, pairs)
            source = lax.rem(pair + pairs - hop, pairs)
            far.append(
                remote(v_ref.at[part], left.at[pair, side, part], {"vec": target * 2 + side})
            )
            relay.append(
                remote(left.at[source, side, part], left.at[source, side, part], sibling)
            )
    rim_copy.start()
    for copy in z_copies:
        copy.start()
    for k in range(chunks):
        for copy in far[k * (pairs - 1) : (k + 1) * (pairs - 1)]:
            copy.start()
        for copy in y_copies[k]:
            copy.start()
    near.start()

    lane = lax.broadcasted_iota(jnp.int32, (1, lanes), 1)
    low_half = lane < width
    last_mask = lax.rem(lane, width) == width - 1
    first_mask = lax.rem(lane, width) == 0
    sign = jnp.where(low_half, 1.0, -1.0).astype(jnp.float32)
    tile = 32 if rows % 32 == 0 else rows

    for copy in scalars:
        copy.wait()
    site_shape = (depth * height, lanes)
    site = lax.broadcasted_iota(jnp.int32, site_shape, 0)
    x_at = lax.rem(lax.broadcasted_iota(jnp.int32, site_shape, 1), width)
    y_at = me_y * height + lax.rem(site, height)
    z_at = me_z * depth + site // height

    def fraction(component, at, extent):
        turned = lax.rem(momentum_ref[component] * at, extent)
        turned = jnp.where(turned < 0, turned + extent, turned)
        return turned.astype(jnp.float32) / extent

    angle = (2.0 * math.pi) * (
        fraction(2, z_at, depth * gz_n)
        + fraction(1, y_at, height * gy_n)
        + fraction(0, x_at, width)
    )
    cos_ref[...] = jnp.cos(angle)
    sin_ref[...] = jnp.sin(angle) * sign

    def coefficients(raw):
        value = raw.astype(jnp.float32) * 0.5
        swapped = pltpu.roll(value, width, 1)
        real = jnp.where(low_half, value, swapped)
        imag = jnp.where(low_half, -swapped, value)
        return real, imag

    def put(table, where, pair_of):
        table[where + (slice(0, 9),)] = pair_of[0]
        table[where + (slice(16, 25),)] = pair_of[1]

    def step_back(value):
        one = pltpu.roll(value, 1, 1)
        two = pltpu.roll(value, width + 1, 1)
        return jnp.where(first_mask, two, one)

    def make_tables(z):
        for y in range(height):
            real, imag = coefficients(links_ref[0, z, y])
            put(tab_x, (0, z, y), (real, imag))
            put(tab_x, (1, z, y), (step_back(real), step_back(imag)))
            put(tab_y, (z, y + 1), coefficients(links_ref[1, z, y]))
            put(tab_z, (z + 1, y), coefficients(links_ref[2, z, y]))

    pl.loop(0, depth)(make_tables)

    def store(z, y, colour, slot, lo, value):
        turned = pltpu.roll(value, width, 1) * sign
        trans[z, y, colour, pl.ds(slot * 2 * rows + lo, tile)] = value.astype(jnp.bfloat16)
        trans[z, y, colour, pl.ds((slot * 2 + 1) * rows + lo, tile)] = turned.astype(jnp.bfloat16)

    def load(z, y, colour, lo):
        return ext[z, y, colour, pl.ds(lo, tile)].astype(jnp.float32)

    def stencil(z, y, lo, slot, ahead, behind, up, down):
        sums = [0.0, 0.0, 0.0]
        for col in range(3):
            value, swapped = ahead(col)
            for row in range(3):
                k = row * 3 + col
                sums[row] = sums[row] + (up(k) * value + up(16 + k) * swapped)
        for col in range(3):
            value, swapped = behind(col)
            for row in range(3):
                k = col * 3 + row
                sums[row] = sums[row] + (down(16 + k) * swapped - down(k) * value)
        for row in range(3):
            store(z, y, row, slot, lo, sums[row])

    def swap(value):
        return value, pltpu.roll(value, width, 1)

    def pass_x(z):
        for y in range(height):
            for lo in range(0, rows, tile):
                here = pl.ds(z * height + y, 1)
                cosine = cos_ref[here]
                sine = sin_ref[here]

                def ahead(col):
                    value = load(z + 1, y + 1, col, lo)
                    one = pltpu.roll(value, lanes - 1, 1)
                    two = pltpu.roll(value, width - 1, 1)
                    return jnp.where(last_mask, two, one), jnp.where(last_mask, one, two)

                def behind(col):
                    value = load(z + 1, y + 1, col, lo)
                    one = pltpu.roll(value, 1, 1)
                    two = pltpu.roll(value, width + 1, 1)
                    return jnp.where(first_mask, two, one), jnp.where(first_mask, one, two)

                stencil(
                    z, y, lo, 0, ahead, behind,
                    lambda k: tab_x[0, z, y, k : k + 1],
                    lambda k: tab_x[1, z, y, k : k + 1],
                )
                for col in range(3):
                    value, swapped = swap(load(z + 1, y + 1, col, lo))
                    store(z, y, col, 2, lo, value * cosine + swapped * sine)

    def pass_y(z):
        for y in range(height):
            for lo in range(0, rows, tile):
                stencil(
                    z, y, lo, 3,
                    lambda col: swap(load(z + 1, y + 2, col, lo)),
                    lambda col: swap(load(z + 1, y, col, lo)),
                    lambda k: tab_y[z, y + 1, k : k + 1],
                    lambda k: tab_y[z, y, k : k + 1],
                )

    def pass_z(z):
        for y in range(height):
            for lo in range(0, rows, tile):
                stencil(
                    z, y, lo, 1,
                    lambda col: swap(load(z + 2, y + 1, col, lo)),
                    lambda col: swap(load(z, y + 1, col, lo)),
                    lambda k: tab_z[z + 1, y, k : k + 1],
                    lambda k: tab_z[z, y, k : k + 1],
                )

    def contract(which, chunk, lo, hi, fresh):
        sites = [
            (chunk * span + dz, y, c) for dz in range(span) for y in range(height) for c in range(3)
        ]
        a = jnp.concatenate([trans[z, y, c, lo:hi] for z, y, c in sites], axis=1)
        b = jnp.concatenate(
            [
                jnp.concatenate([left[which, s, z, y, c] for z, y, c in sites], axis=1)
                for s in range(2)
            ],
            axis=0,
        )
        product = lax.dot_general(
            a, b, (((1,), (1,)), ((), ())), preferred_element_type=jnp.float32
        )
        columns = pl.ds(pl.multiple_of(which * 2 * rows, 2 * rows), 2 * rows)
        if fresh:
            acc[lo:hi, columns] = product
        else:
            acc[lo:hi, columns] += product

    for copy in locals_:
        copy.wait()
    pl.loop(0, depth)(pass_x)
    for copy in z_copies:
        copy.wait()
    for y in range(height):
        put(tab_z, (0, y), coefficients(rim_z[y]))
    pl.loop(0, depth)(pass_z)

    early = 6 * rows
    near.wait()
    contract(pair, 0, 0, early, True)
    pl.loop(1, chunks)(lambda k: contract(pair, k, 0, early, False))

    own_columns = pl.ds(pl.multiple_of(pair * 2 * rows, 2 * rows), 2 * rows)
    stages = [
        [(own_columns, 0, early)],
        [
            (
                pl.ds(
                    pl.multiple_of(lax.rem(pair + pairs - hop, pairs) * 2 * rows, 2 * rows),
                    2 * rows,
                ),
                0,
                8 * rows,
            )
            for hop in range(1, pairs)
        ]
        + [(own_columns, early, 8 * rows)],
    ]

    def exchange(stage, phase, step):
        source = outgo[stage].at[member(step)] if phase == 0 else reduced[stage]
        target = income[stage] if phase == 0 else gathered[stage]
        return pltpu.make_async_remote_copy(
            src_ref=source,
            dst_ref=target.at[me_g],
            send_sem=red_sem.at[stage, phase, 0, step],
            recv_sem=red_sem.at[stage, phase, 1, step],
            device_id=place(member(step)),
            device_id_type=MESH,
        )

    def pieces(stage):
        at = 0
        for columns, lo, hi in stages[stage]:
            share = (hi - lo) // group
            yield columns, lo, share, at
            at += share

    def scatter_start(stage):
        for columns, lo, share, at in pieces(stage):
            for g in range(group):
                outgo[stage][g, at : at + share] = acc[
                    lo + g * share : lo + (g + 1) * share, columns
                ].astype(jnp.bfloat16)
        for step in range(1, group):
            exchange(stage, 0, step).start()

    def gather_start(stage):
        for step in range(1, group):
            exchange(stage, 0, step).wait()
        total = outgo[stage][me_g].astype(jnp.float32)
        for step in range(1, group):
            total = total + income[stage][member(step)].astype(jnp.float32)
        reduced[stage][...] = total.astype(jnp.bfloat16)
        gathered[stage][me_g] = total.astype(jnp.bfloat16)
        for step in range(1, group):
            exchange(stage, 1, step).start()

    def gather_finish(stage):
        for step in range(1, group):
            exchange(stage, 1, step).wait()
        for columns, lo, share, at in pieces(stage):
            for g in range(group):
                acc[lo + g * share : lo + (g + 1) * share, columns] = gathered[stage][
                    g, at : at + share
                ].astype(jnp.float32)

    scatter_start(0)
    rim_copy.wait()

    @pl.loop(0, depth)
    def _(z):
        put(tab_y, (z, 0), coefficients(rim_y[z]))

    for k in range(chunks + 1):
        if k < chunks:
            for hop in range(1, pairs):
                index = k * (pairs - 1) + hop - 1
                far[index].wait()
                relay[index].start()
            for copy in y_copies[k]:
                copy.wait()
            pl.loop(k * span, (k + 1) * span)(pass_y)
            contract(pair, k, early, 8 * rows, k == 0)
        if k == chunks - 1:
            gather_start(0)
        if k:
            for hop in range(1, pairs):
                relay[(k - 1) * (pairs - 1) + hop - 1].wait()
                contract(lax.rem(pair + pairs - hop, pairs), k - 1, 0, 8 * rows, k == 1)

    scatter_start(1)
    gather_start(1)
    gather_finish(0)
    gather_finish(1)

    scale = 1.0 / math.sqrt(width * height * gy_n * depth * gz_n)
    full = acc[...] * scale
    along_x, along_z, phased, along_y = [
        full[slot * 2 * rows : (slot + 1) * 2 * rows] for slot in range(4)
    ]
    for slot in range(3):
        chosen = directions_ref[slot]
        out_ref[slot * 2 * rows : (slot + 1) * 2 * rows] = jnp.where(
            chosen == 0, along_x, jnp.where(chosen == 1, along_y, along_z)
        )
    out_ref[6 * rows :] = phased


def body(vectors, links, momentum, directions):
    rows, _, depth, height, lanes = vectors.shape
    gz_n = lax.axis_size("gz")
    gy_n = lax.axis_size("gy")
    vec_n = lax.axis_size("vec")
    group = gz_n * gy_n
    chunks = split_chunks(depth, 4)
    v = jnp.transpose(vectors, (2, 3, 1, 0, 4))
    packed = jnp.transpose(links, (0, 3, 4, 1, 2, 5)).reshape(3, depth, height, 9, lanes)

    bf16, f32 = jnp.bfloat16, jnp.float32
    pairs = vec_n // 2
    shares = (6 * rows // group, (8 * (pairs - 1) + 2) * rows // group)
    remote_count = 5 + chunks * (2 + 2 * (pairs - 1))
    vmem = pl.BlockSpec(memory_space=pltpu.VMEM)
    hbm = pl.BlockSpec(memory_space=pl.ANY)
    sizes = (gz_n, gy_n, vec_n, depth, height, rows, lanes // 2, chunks)
    out = pl.pallas_call(
        functools.partial(kernel, sizes),
        out_shape=jax.ShapeDtypeStruct((8 * rows, vec_n * rows), f32),
        in_specs=[hbm, hbm, hbm, vmem, hbm],
        out_specs=vmem,
        scratch_shapes=[
            pltpu.VMEM((depth + 2, height + 2, 3, rows, lanes), bf16),
            pltpu.VMEM((pairs, 2, depth, height, 3, rows, lanes), bf16),
            pltpu.VMEM((depth, 9, lanes), bf16),
            pltpu.VMEM((height, 9, lanes), bf16),
            pltpu.VMEM((2, depth, height, 32, lanes), f32),
            pltpu.VMEM((depth, height + 1, 32, lanes), f32),
            pltpu.VMEM((depth + 1, height, 32, lanes), f32),
            pltpu.VMEM((depth * height, lanes), f32),
            pltpu.VMEM((depth * height, lanes), f32),
            pltpu.VMEM((depth, height, 3, 8 * rows, lanes), bf16),
            pltpu.VMEM((8 * rows, vec_n * rows), f32),
            pltpu.SMEM((3,), jnp.int32),
            pltpu.SMEM((3,), jnp.int32),
            [pltpu.VMEM((group, share, 2 * rows), bf16) for share in shares],
            [pltpu.VMEM((group, share, 2 * rows), bf16) for share in shares],
            [pltpu.VMEM((share, 2 * rows), bf16) for share in shares],
            [pltpu.VMEM((group, share, 2 * rows), bf16) for share in shares],
            pltpu.SemaphoreType.DMA((4,)),
            pltpu.SemaphoreType.DMA((remote_count,)),
            pltpu.SemaphoreType.DMA((remote_count,)),
            pltpu.SemaphoreType.DMA((2, 2, 2, group)),
        ],
        compiler_params=pltpu.CompilerParams(
            collective_id=0, has_side_effects=True, vmem_limit_bytes=48 * 1024 * 1024
        ),
    )(momentum, directions, v, packed, packed)
    return out.reshape(4, 2, rows, vec_n * rows)


def solution(mesh):
    in_specs = (P("vec", None, "gz", "gy", None), P(None, None, None, "gz", "gy", None), P(), P())
    out_specs = P(None, None, "vec", None)
    return jax.shard_map(body, mesh=mesh, in_specs=in_specs, out_specs=out_specs, check_vma=False)
```
